32 devices in a mesh: row: 4 (over y, x), col: 8 (over z, core).
Axes of the slice: x: 2, y: 2, z: 4, core: 2. Of those that a mesh axis runs over, the one named last changes fastest.
Arguments:
- sim: bfloat16 [8192, 8192], P('row', 'col'), may hold values from -6 to 6
- diag_blocks: bfloat16 [2048, 8192], P(None, 'col'), may hold values from -0.125 to 0.125
- match_perm: int32 [4, 2048], replicated, may hold values from 0 to 2047, each once within a row
- match_scale: float32 [4, 2048], replicated, may hold values from 0.3 to 1.5
- features: bfloat16 [8192, 256], P('col'), may hold values from -0.0625 to 0.0625
Outputs:
- new_sim: bfloat16 [8192, 8192], P('row', 'col')
- aggregated: float32 [8192, 256], P(('row', 'col'))
The draws below stay inside these ranges and needn't reach their ends.
Inputs may be any that keep to these rules, and one draw needn't show every extreme that they name: Each row of match_perm lists every number of 0 to 2047 once.
All inputs are finite; a program needn't handle non-finite values.
Results may differ from the reference program's by a relative error of at most 0.0058.
Values may be sent and summed in bfloat16 or wider, within the bound.
No kernel may reach another device: no remote copies, remote signals or barrier semaphores. Data moves between devices by JAX's collectives and lax.ppermute only.
A program may use at most 128 MiB of HBM per device.

```python
import math
import jax
import jax.numpy as jnp
from jax import lax

NB = 2048
F = 256
K = 4
N = 8192
N_COL = 8


def steps_of(own_key, shape, shards, smallest, top_value):
    level, own = 1.0, jax.random.fold_in(own_key, 6)
    for dim, blocks in shards:
        steps = jnp.exp(jax.random.uniform(jax.random.fold_in(own, dim), (blocks,), jnp.float32, smallest / len(shards), top_value / len(shards)))
        level = level * jnp.repeat(steps, shape[dim] // blocks).reshape([-1 if axis == dim else 1 for axis in range(len(shape))])
    return level


def scatter_about(key, extent, deviation, limit, shards=(), kind=jnp.bfloat16):
    result = deviation * jax.random.normal(key, extent, jnp.float32)
    if shards:
        result = result * steps_of(key, extent, shards, -0.22, 0.18)
    return jnp.clip(result, -limit, limit).astype(kind)


def setup_inputs(seed: int = 0) -> dict:
    seeds = jax.random.split(jax.random.key(seed), 6)
    sim = scatter_about(seeds[0], (N, N), 1.0, 6.0, ((0, 4), (1, 8)))
    diag_blocks = scatter_about(seeds[1], (NB, N), NB ** -0.5, 0.125, ((1, 8),))
    match_perm = jax.vmap(lambda own: jax.random.permutation(own, NB))(jax.random.split(seeds[2], K)).reshape((K, NB)).astype(jnp.int32)
    match_scale = jnp.clip(jnp.exp(jax.random.uniform(seeds[3], (K, NB), jnp.float32, math.log(0.3), math.log(1.5))), 0.3, 1.5)
    features = scatter_about(seeds[4], (N, F), N ** -0.5, 0.0625, ((0, 8),))
    return {"sim": sim, "diag_blocks": diag_blocks, "match_perm": match_perm, "match_scale": match_scale, "features": features}


decay_factor = 0.8


def reference(sim, diag_blocks, match_perm, match_scale, features):
    blocks = N_COL // 2
    halfway = blocks // 2
    total = NB * blocks
    columns = []
    for target in range(blocks):
        source = (target + halfway) % blocks
        own_part = sim[:, target * NB:(target + 1) * NB]
        far_part = sim[:, source * NB:(source + 1) * NB]
        moved = (jnp.take(far_part, match_perm[source], axis=1) * match_scale[source][None, :]).astype(jnp.bfloat16)
        product = jnp.dot(own_part, diag_blocks[:, target * NB:(target + 1) * NB], preferred_element_type=jnp.float32)
        columns.append((product + moved).astype(jnp.bfloat16))
    mixed = jnp.concatenate(columns, axis=1)
    row_blocks = []
    for target in range(blocks):
        source = (target + halfway) % blocks
        own_rows = mixed[target * NB:(target + 1) * NB]
        far_rows = mixed[source * NB:(source + 1) * NB]
        moved = (jnp.take(far_rows, match_perm[source], axis=0) * match_scale[source][:, None]).astype(jnp.bfloat16)
        product = lax.dot_general(diag_blocks[:, target * NB:(target + 1) * NB], own_rows, (((0,), (0,)), ((), ())), preferred_element_type=jnp.float32)
        row_blocks.append((decay_factor * (product + moved)).astype(jnp.bfloat16))
    new_sim = jnp.concatenate(row_blocks, axis=0)
    index = jnp.arange(total)
    new_sim = new_sim.at[index, index].set(jnp.ones((total,), new_sim.dtype))
    aggregated = jnp.dot(new_sim, features, preferred_element_type=jnp.float32)
    return new_sim, aggregated
```

```python
import jax
import jax.numpy as jnp
from jax import lax
from jax.experimental import pallas as pl
from jax.experimental.pallas import tpu as pltpu
from jax.sharding import PartitionSpec as P


decay_factor = 0.8
parts = (2, 2, 2, 2, 2, 2, 2, 1, 1)
groups = ((0, 4), (4, 6))


def flipped(value, axis, mask):
    pairs = [(source, source ^ mask) for source in range(lax.axis_size(axis))]
    return lax.ppermute(value, axis, pairs)


def shifted(value, axis, steps):
    count = lax.axis_size(axis)
    pairs = [(source, (source + steps) % count) for source in range(count)]
    return lax.ppermute(value, axis, pairs)


def dot(a, b):
    return jnp.dot(a, b, preferred_element_type=jnp.float32)


def dot_t(a, b):
    return lax.dot_general(a, b, (((0,), (0,)), ((), ())), preferred_element_type=jnp.float32)


def one_hot(start, rows, targets):
    index = start + lax.broadcasted_iota(jnp.int32, (rows, targets.shape[0]), 0)
    return (index == targets[None, :]).astype(jnp.bfloat16)


def part(x, start, size, axis=0):
    return lax.dynamic_slice_in_dim(x, start, size, axis)


def pick(items, index):
    result = items[0]
    for position in range(1, len(items)):
        result = jnp.where(index == position, items[position], result)
    return result


def tile_product(refs, kept, h, start):
    b_own, b_par, perm, scale = refs
    near, far = kept
    shape = (perm.shape[1], near.shape[0])
    index = start + lax.broadcasted_iota(jnp.int32, shape, 1)
    chosen = (index == perm[0]).astype(jnp.bfloat16)
    moved = dot(chosen, far[...]) * scale[0]
    return moved + dot_t(jnp.where(h == 0, b_own[...], b_par[...]), near[...])


def keep(chunks, kept):
    @pl.when((pl.program_id(0) == 0) & (pl.program_id(1) == 0))
    def _():
        start = 0
        for pair in chunks:
            depth = pair[0].shape[0]
            for one, whole in zip(pair, kept):
                whole[start : start + depth] = one[...]
            start += depth


def tile_specs(start, depth, chunks, tile, tiles, at):
    wide = chunks[0][0].shape[1]
    last = at(tiles - 1)
    specs = [
        pl.BlockSpec((depth, tile), lambda h, i, *_: (start // depth, jnp.where(h == 0, at(i), last))),
        pl.BlockSpec((depth, tile), lambda h, i, *_: (start // depth, jnp.where(h == 0, at(0), at(i)))),
        pl.BlockSpec((1, tile, 1), lambda h, i, *_: (h, at(i), 0)),
        pl.BlockSpec((1, tile, 1), lambda h, i, *_: (h, at(i), 0)),
    ]
    for near, _ in chunks:
        specs += [pl.BlockSpec((near.shape[0], wide), lambda h, i, *_: (0, 0))] * 2
    return specs


def paired(refs, count):
    return [(refs[2 * n], refs[2 * n + 1]) for n in range(count)]


def flat(chunks):
    return [one for pair in chunks for one in pair]


def accumulate(halves, perm, scale, chunks, start, total):
    tall = halves[0].shape[1]
    wide = chunks[0][0].shape[1]
    depth = sum(near.shape[0] for near, _ in chunks)
    tile = min(512, tall)
    count = len(chunks)

    def body(*refs):
        kept = refs[-2:]
        out = refs[-3]
        keep(paired(refs[4:], count), kept)
        result = tile_product(refs[:4], kept, pl.program_id(0), start)
        if total is not None:
            result = result + refs[-4][0]
        out[0] = result

    place = pl.BlockSpec((1, tile, wide), lambda h, i: (h, i, 0))
    specs = tile_specs(start, depth, chunks, tile, tall // tile, lambda i: i)
    operands = [*halves, perm, scale, *flat(chunks)]
    if total is not None:
        specs.append(place)
        operands.append(total)
    return pl.pallas_call(
        body,
        out_shape=jax.ShapeDtypeStruct((2, tall, wide), jnp.float32),
        grid=(2, tall // tile),
        in_specs=specs,
        out_specs=place,
        scratch_shapes=[pltpu.VMEM((depth, wide), jnp.bfloat16)] * 2,
        input_output_aliases={} if total is None else {len(operands) - 1: 0},
        compiler_params=pltpu.CompilerParams(vmem_limit_bytes=58 * 2**20),
        name="accumulate",
    )(*operands)


def finish(halves, perm, scale, chunks, start, total, features, origin):
    tall = halves[0].shape[1]
    wide = chunks[0][0].shape[1]
    depth = sum(near.shape[0] for near, _ in chunks)
    tile = min(512, tall)
    tiles = tall // tile
    count = len(chunks)

    def body(origin_ref, *refs):
        h = pl.program_id(0)
        total_ref, feature_ref, sim_ref, sum_ref, *kept = refs[4 + 2 * count :]
        keep(paired(refs[4:], count), kept)
        result = tile_product(refs[:4], kept, h, start) + total_ref[0]
        place = jnp.where(h == 0, origin_ref[0], 1 - origin_ref[0])
        row = origin_ref[1] + place * tall + pl.program_id(1) * tile
        row = row + lax.broadcasted_iota(jnp.int32, result.shape, 0)
        col = origin_ref[2] + lax.broadcasted_iota(jnp.int32, result.shape, 1)
        done = jnp.where(row == col, 1.0, decay_factor * result).astype(jnp.bfloat16)
        sim_ref[...] = done
        sum_ref[...] = dot(done, feature_ref[...])

    def placed(h, i, o):
        return (jnp.where(h == 0, o[0], 1 - o[0]) * tiles + i, 0)

    specs = tile_specs(start, depth, chunks, tile, tiles, lambda i: i)
    specs += [
        pl.BlockSpec((1, tile, wide), lambda h, i, o: (h, i, 0)),
        pl.BlockSpec(features.shape, lambda h, i, o: (0, 0)),
    ]
    operands = [*halves, perm, scale, *flat(chunks), total, features]
    return pl.pallas_call(
        body,
        out_shape=(
            jax.ShapeDtypeStruct((2 * tall, wide), jnp.bfloat16),
            jax.ShapeDtypeStruct((2 * tall, features.shape[1]), jnp.float32),
        ),
        grid_spec=pltpu.PrefetchScalarGridSpec(
            num_scalar_prefetch=1,
            grid=(2, tiles),
            in_specs=specs,
            out_specs=(
                pl.BlockSpec((tile, wide), placed),
                pl.BlockSpec((tile, features.shape[1]), placed),
            ),
            scratch_shapes=[pltpu.VMEM((depth, wide), jnp.bfloat16)] * 2,
        ),
        compiler_params=pltpu.CompilerParams(vmem_limit_bytes=58 * 2**20),
        name="finish",
    )(origin, *operands)


def gathered_block(diag_blocks, row_id, block_id, row_count, block_count):
    cols = 2 * block_count
    slice_rows = diag_blocks.shape[0] // row_count
    own = part(diag_blocks, row_id * slice_rows, slice_rows)
    ups, downs = [own], [own]
    for step in range(1, block_count):
        up_pairs = [(c, c + 2) for c in range(cols - 2) if c // 2 >= step - 1]
        down_pairs = [(c, c - 2) for c in range(2, cols) if c // 2 + step - 1 <= block_count - 1]
        ups.append(lax.ppermute(ups[-1], "col", up_pairs))
        downs.append(lax.ppermute(downs[-1], "col", down_pairs))
    slices = [own] + [ups[j] + downs[block_count - j] for j in range(1, block_count)]
    whole = jnp.zeros(diag_blocks.shape, diag_blocks.dtype)
    for distance in range(row_count):
        wanted = row_id ^ distance
        piece = pick(slices, (block_id - wanted) % block_count)
        if distance:
            piece = flipped(piece, "row", distance)
        whole = lax.dynamic_update_slice_in_dim(whole, piece, wanted * slice_rows, 0)
    return whole


def program(sim, diag_blocks, match_perm, match_scale, features):
    row_count = lax.axis_size("row")
    col_count = lax.axis_size("col")
    block_count = col_count // 2
    row_id = lax.axis_index("row")
    col_id = lax.axis_index("col")
    block_id = col_id // 2
    side = col_id % 2
    rows, half = sim.shape
    other = 1 - side
    bf16 = jnp.bfloat16
    spans = [(sum(parts[:n]) * rows // 16, parts[n] * rows // 16) for n in range(len(parts))]

    whole_b = gathered_block(diag_blocks, row_id, block_id, row_count, block_count)
    partner = flipped(sim, "col", 1)

    far_block = (block_id + block_count // 2) % block_count
    far_row = (row_id + row_count // 2) % row_count
    perm_c = part(lax.dynamic_index_in_dim(match_perm, far_block, 0, False), side * half, half)
    scale_c = part(lax.dynamic_index_in_dim(match_scale, far_block, 0, False), side * half, half)
    perm_r = lax.dynamic_index_in_dim(match_perm, far_row, 0, False)
    scale_r = lax.dynamic_index_in_dim(match_scale, far_row, 0, False)
    perm_r = jnp.stack([part(perm_r, side * half, half), part(perm_r, other * half, half)])
    scale_r = jnp.stack([part(scale_r, side * half, half), part(scale_r, other * half, half)])
    pick_own = one_hot(side * half, half, perm_c)
    pick_par = one_hot(other * half, half, perm_c)
    perm_r = perm_r[:, :, None]
    scale_r = scale_r[:, :, None]
    b_own = part(diag_blocks, side * half, half)
    b_par = part(diag_blocks, other * half, half)

    local = dot(sim, b_own)
    local = local + dot(partner, b_par)
    cuts = [sim[start : start + depth] for start, depth in spans]
    chunks = []
    for n, (start, depth) in enumerate(spans):
        span = slice(start, start + depth)
        got = shifted(cuts[n], "col", col_count // 2)
        got_par = flipped(got, "col", 1)
        moved = dot(got, pick_own) + dot(got_par, pick_par)
        mixed = (local[span] + moved * scale_c[None, :]).astype(bf16)
        chunks.append((mixed, shifted(mixed, "row", row_count // 2)))

    other_b = flipped(whole_b, "col", 1)
    halves = (whole_b, other_b)
    total = None
    for low, high in groups:
        total = accumulate(
            halves, perm_r, scale_r, chunks[low:high], spans[low][0], total
        )

    low = groups[-1][1]
    origin = jnp.stack([side, row_id * rows, col_id * half]).astype(jnp.int32)
    new_sim, sums = finish(
        halves, perm_r, scale_r, chunks[low:], spans[low][0], total,
        features, origin,
    )
    aggregated = scattered(sums, side, block_id, block_count)
    return new_sim, aggregated


def scattered(total, side, block_id, block_count):
    total = total.reshape(block_count, 2, -1, total.shape[1])
    kept = lax.dynamic_index_in_dim(total, side, 1, False)
    sent = lax.dynamic_index_in_dim(total, 1 - side, 1, False).astype(jnp.bfloat16)
    kept = kept + flipped(sent, "col", 1)
    result = lax.dynamic_index_in_dim(kept, block_id, 0, False)
    for distance in range(1, block_count):
        sent = lax.dynamic_index_in_dim(kept, block_id ^ distance, 0, False)
        result = result + flipped(sent.astype(jnp.bfloat16), "col", 2 * distance)
    return result


def solution(mesh):
    placed = (P("row", "col"), P(None, "col"), P(), P(), P("col", None))
    return jax.shard_map(
        program,
        mesh=mesh,
        in_specs=placed,
        out_specs=(P("row", "col"), P(("row", "col"), None)),
        check_vma=False,
    )
```

```python
import jax
import jax.numpy as jnp
from jax import lax
from jax.experimental import pallas as pl
from jax.experimental.pallas import tpu as pltpu
from jax.sharding import PartitionSpec as P


decay_factor = 0.8
parts = (2, 2, 2, 2, 2, 2, 2, 1, 1)
groups = ((0, 3), (3, 6))
pieces = 2


def flipped(value, axis, mask):
    pairs = [(source, source ^ mask) for source in range(lax.axis_size(axis))]
    return lax.ppermute(value, axis, pairs)


def shifted(value, axis, steps):
    count = lax.axis_size(axis)
    pairs = [(source, (source + steps) % count) for source in range(count)]
    return lax.ppermute(value, axis, pairs)


def dot(a, b):
    return jnp.dot(a, b, preferred_element_type=jnp.float32)


def dot_t(a, b):
    return lax.dot_general(a, b, (((0,), (0,)), ((), ())), preferred_element_type=jnp.float32)


def one_hot(start, rows, targets):
    index = start + lax.broadcasted_iota(jnp.int32, (rows, targets.shape[0]), 0)
    return (index == targets[None, :]).astype(jnp.bfloat16)


def part(x, start, size, axis=0):
    return lax.dynamic_slice_in_dim(x, start, size, axis)


def pick(items, index):
    result = items[0]
    for position in range(1, len(items)):
        result = jnp.where(index == position, items[position], result)
    return result


def tile_product(refs, kept, h, start):
    b_own, b_par, perm, scale = refs
    near, far = kept
    shape = (perm.shape[1], near.shape[0])
    index = start + lax.broadcasted_iota(jnp.int32, shape, 1)
    chosen = (index == perm[0]).astype(jnp.bfloat16)
    moved = dot(chosen, far[...]) * scale[0]
    return moved + dot_t(jnp.where(h == 0, b_own[...], b_par[...]), near[...])


def keep(chunks, kept):
    @pl.when((pl.program_id(0) == 0) & (pl.program_id(1) == 0))
    def _():
        start = 0
        for pair in chunks:
            depth = pair[0].shape[0]
            for one, whole in zip(pair, kept):
                whole[start : start + depth] = one[...]
            start += depth


def tile_specs(start, depth, chunks, tile, tiles, at):
    wide = chunks[0][0].shape[1]
    last = at(tiles - 1)
    specs = [
        pl.BlockSpec((depth, tile), lambda h, i, *_: (start // depth, jnp.where(h == 0, at(i), last))),
        pl.BlockSpec((depth, tile), lambda h, i, *_: (start // depth, jnp.where(h == 0, at(0), at(i)))),
        pl.BlockSpec((1, tile, 1), lambda h, i, *_: (h, at(i), 0)),
        pl.BlockSpec((1, tile, 1), lambda h, i, *_: (h, at(i), 0)),
    ]
    for near, _ in chunks:
        specs += [pl.BlockSpec((near.shape[0], wide), lambda h, i, *_: (0, 0))] * 2
    return specs


def paired(refs, count):
    return [(refs[2 * n], refs[2 * n + 1]) for n in range(count)]


def flat(chunks):
    return [one for pair in chunks for one in pair]


def accumulate(halves, perm, scale, chunks, start, total):
    tall = halves[0].shape[1]
    wide = chunks[0][0].shape[1]
    depth = sum(near.shape[0] for near, _ in chunks)
    tile = min(512, tall)
    count = len(chunks)

    def body(*refs):
        kept = refs[-2:]
        out = refs[-3]
        keep(paired(refs[4:], count), kept)
        result = tile_product(refs[:4], kept, pl.program_id(0), start)
        if total is not None:
            result = result + refs[-4][0]
        out[0] = result

    place = pl.BlockSpec((1, tile, wide), lambda h, i: (h, i, 0))
    specs = tile_specs(start, depth, chunks, tile, tall // tile, lambda i: i)
    operands = [*halves, perm, scale, *flat(chunks)]
    if total is not None:
        specs.append(place)
        operands.append(total)
    return pl.pallas_call(
        body,
        out_shape=jax.ShapeDtypeStruct((2, tall, wide), jnp.float32),
        grid=(2, tall // tile),
        in_specs=specs,
        out_specs=place,
        scratch_shapes=[pltpu.VMEM((depth, wide), jnp.bfloat16)] * 2,
        input_output_aliases={} if total is None else {len(operands) - 1: 0},
        compiler_params=pltpu.CompilerParams(vmem_limit_bytes=58 * 2**20),
        name="accumulate",
    )(*operands)


def finish(halves, perm, scale, chunks, start, total, features, origin):
    tall = halves[0].shape[1]
    wide = chunks[0][0].shape[1]
    depth = sum(near.shape[0] for near, _ in chunks)
    tile = min(512, tall)
    tiles = tall // tile
    count = len(chunks)

    def body(origin_ref, *refs):
        h = pl.program_id(0)
        total_ref, feature_ref, sim_ref, sum_ref, *kept = refs[4 + 2 * count :]
        keep(paired(refs[4:], count), kept)
        result = tile_product(refs[:4], kept, h, start) + total_ref[0]
        place = jnp.where(h == 0, origin_ref[0], 1 - origin_ref[0])
        row = origin_ref[1] + place * tall + pl.program_id(1) * tile
        row = row + lax.broadcasted_iota(jnp.int32, result.shape, 0)
        col = origin_ref[2] + lax.broadcasted_iota(jnp.int32, result.shape, 1)
        done = jnp.where(row == col, 1.0, decay_factor * result).astype(jnp.bfloat16)
        sim_ref[...] = done
        sum_ref[...] = dot(done, feature_ref[...])

    def placed(h, i, o):
        return (jnp.where(h == 0, o[0], 1 - o[0]) * tiles + i, 0)

    specs = tile_specs(start, depth, chunks, tile, tiles, lambda i: i)
    specs += [
        pl.BlockSpec((1, tile, wide), lambda h, i, o: (h, i, 0)),
        pl.BlockSpec(features.shape, lambda h, i, o: (0, 0)),
    ]
    operands = [*halves, perm, scale, *flat(chunks), total, features]
    return pl.pallas_call(
        body,
        out_shape=(
            jax.ShapeDtypeStruct((2 * tall, wide), jnp.bfloat16),
            jax.ShapeDtypeStruct((2 * tall, features.shape[1]), jnp.float32),
        ),
        grid_spec=pltpu.PrefetchScalarGridSpec(
            num_scalar_prefetch=1,
            grid=(2, tiles),
            in_specs=specs,
            out_specs=(
                pl.BlockSpec((tile, wide), placed),
                pl.BlockSpec((tile, features.shape[1]), placed),
            ),
            scratch_shapes=[pltpu.VMEM((depth, wide), jnp.bfloat16)] * 2,
        ),
        compiler_params=pltpu.CompilerParams(vmem_limit_bytes=58 * 2**20),
        name="finish",
    )(origin, *operands)


def gathered_block(diag_blocks, row_id, block_id, row_count, block_count):
    cols = 2 * block_count
    slice_rows = diag_blocks.shape[0] // row_count
    depth = slice_rows // pieces
    whole = jnp.zeros(diag_blocks.shape, diag_blocks.dtype)
    placed = []
    for n in range(pieces):
        own = part(diag_blocks, row_id * slice_rows + n * depth, depth)
        ups, downs = [own], [own]
        for step in range(1, block_count):
            up_pairs = [(c, c + 2) for c in range(cols - 2) if c // 2 >= step - 1]
            down_pairs = [(c, c - 2) for c in range(2, cols) if c // 2 + step - 1 <= block_count - 1]
            ups.append(lax.ppermute(ups[-1], "col", up_pairs))
            downs.append(lax.ppermute(downs[-1], "col", down_pairs))
        slices = [own] + [ups[j] + downs[block_count - j] for j in range(1, block_count)]
        for distance in range(row_count):
            wanted = row_id ^ distance
            piece = pick(slices, (block_id - wanted) % block_count)
            if distance:
                piece = flipped(piece, "row", distance)
            placed.append((distance, n, piece, wanted * slice_rows + n * depth))
    for _, _, piece, place in sorted(placed, key=lambda entry: entry[0] > 0):
        whole = lax.dynamic_update_slice_in_dim(whole, piece, place, 0)
    return whole


def program(sim, diag_blocks, match_perm, match_scale, features):
    row_count = lax.axis_size("row")
    col_count = lax.axis_size("col")
    block_count = col_count // 2
    row_id = lax.axis_index("row")
    col_id = lax.axis_index("col")
    block_id = col_id // 2
    side = col_id % 2
    rows, half = sim.shape
    other = 1 - side
    bf16 = jnp.bfloat16
    spans = [(sum(parts[:n]) * rows // 16, parts[n] * rows // 16) for n in range(len(parts))]

    whole_b = gathered_block(diag_blocks, row_id, block_id, row_count, block_count)
    partner = flipped(sim, "col", 1)

    far_block = (block_id + block_count // 2) % block_count
    far_row = (row_id + row_count // 2) % row_count
    perm_c = part(lax.dynamic_index_in_dim(match_perm, far_block, 0, False), side * half, half)
    scale_c = part(lax.dynamic_index_in_dim(match_scale, far_block, 0, False), side * half, half)
    perm_r = lax.dynamic_index_in_dim(match_perm, far_row, 0, False)
    scale_r = lax.dynamic_index_in_dim(match_scale, far_row, 0, False)
    perm_r = jnp.stack([part(perm_r, side * half, half), part(perm_r, other * half, half)])
    scale_r = jnp.stack([part(scale_r, side * half, half), part(scale_r, other * half, half)])
    pick_own = one_hot(side * half, half, perm_c)
    pick_par = one_hot(other * half, half, perm_c)
    scale_rows = jnp.broadcast_to(scale_c[None, :], (max(d for _, d in spans), half))
    perm_r = perm_r[:, :, None]
    scale_r = scale_r[:, :, None]
    b_own = part(diag_blocks, side * half, half)
    b_par = part(diag_blocks, other * half, half)

    local = dot(sim, b_own)
    local = local + dot(partner, b_par)
    cuts = [sim[start : start + depth] for start, depth in spans]
    chunks = []
    for n, (start, depth) in enumerate(spans):
        span = slice(start, start + depth)
        got = shifted(cuts[n], "col", col_count // 2)
        got_par = flipped(got, "col", 1)
        moved = dot(got, pick_own) + dot(got_par, pick_par)
        mixed = (local[span] + moved * scale_rows[:depth]).astype(bf16)
        chunks.append((mixed, shifted(mixed, "row", row_count // 2)))

    other_b = flipped(whole_b, "col", 1)
    halves = (whole_b, other_b)
    total = None
    for low, high in groups:
        total = accumulate(
            halves, perm_r, scale_r, chunks[low:high], spans[low][0], total
        )

    low = groups[-1][1]
    origin = jnp.stack([side, row_id * rows, col_id * half]).astype(jnp.int32)
    new_sim, sums = finish(
        halves, perm_r, scale_r, chunks[low:], spans[low][0], total,
        features, origin,
    )
    aggregated = scattered(sums, side, block_id, block_count)
    return new_sim, aggregated


def scattered(total, side, block_id, block_count):
    total = total.reshape(block_count, 2, -1, total.shape[1])
    kept = lax.dynamic_index_in_dim(total, side, 1, False)
    sent = lax.dynamic_index_in_dim(total, 1 - side, 1, False).astype(jnp.bfloat16)
    kept = kept + flipped(sent, "col", 1)
    result = lax.dynamic_index_in_dim(kept, block_id, 0, False)
    for distance in range(1, block_count):
        sent = lax.dynamic_index_in_dim(kept, block_id ^ distance, 0, False)
        result = result + flipped(sent.astype(jnp.bfloat16), "col", 2 * distance)
    return result


def solution(mesh):
    placed = (P("row", "col"), P(None, "col"), P(), P(), P("col", None))
    return jax.shard_map(
        program,
        mesh=mesh,
        in_specs=placed,
        out_specs=(P("row", "col"), P(("row", "col"), None)),
        check_vma=False,
    )
```

```python
import jax
import jax.numpy as jnp
from jax import lax
from jax.experimental import pallas as pl
from jax.experimental.pallas import tpu as pltpu
from jax.sharding import PartitionSpec as P


decay_factor = 0.8
parts = (2,) * 8
groups = ((0, 6),)
first_quarters = 3
pieces = 2


def flipped(value, axis, mask):
    pairs = [(source, source ^ mask) for source in range(lax.axis_size(axis))]
    return lax.ppermute(value, axis, pairs)


def shifted(value, axis, steps):
    count = lax.axis_size(axis)
    pairs = [(source, (source + steps) % count) for source in range(count)]
    return lax.ppermute(value, axis, pairs)


def dot(a, b):
    return jnp.dot(a, b, preferred_element_type=jnp.float32)


def dot_t(a, b):
    return lax.dot_general(a, b, (((0,), (0,)), ((), ())), preferred_element_type=jnp.float32)


def one_hot(start, rows, targets):
    index = start + lax.broadcasted_iota(jnp.int32, (rows, targets.shape[0]), 0)
    return (index == targets[None, :]).astype(jnp.bfloat16)


def part(x, start, size, axis=0):
    return lax.dynamic_slice_in_dim(x, start, size, axis)


def pick(items, index):
    result = items[0]
    for position in range(1, len(items)):
        result = jnp.where(index == position, items[position], result)
    return result


def tile_product(refs, kept, h, start):
    b_own, b_par, perm, scale = refs
    near, far = kept
    shape = (perm.shape[1], near.shape[0])
    index = start + lax.broadcasted_iota(jnp.int32, shape, 1)
    chosen = (index == perm[0]).astype(jnp.bfloat16)
    moved = dot(chosen, far[...]) * scale[0]
    return moved + dot_t(jnp.where(h == 0, b_own[...], b_par[...]), near[...])


def keep(chunks, kept):
    @pl.when((pl.program_id(0) == 0) & (pl.program_id(1) == 0))
    def _():
        start = 0
        for pair in chunks:
            depth = pair[0].shape[0]
            for one, whole in zip(pair, kept):
                whole[start : start + depth] = one[...]
            start += depth


def tile_specs(start, depth, chunks, tile, tiles, at):
    wide = chunks[0][0].shape[1]
    last = at(tiles - 1)
    specs = [
        pl.BlockSpec((depth, tile), lambda h, i, *_: (start // depth, jnp.where(h == 0, at(i), last))),
        pl.BlockSpec((depth, tile), lambda h, i, *_: (start // depth, jnp.where(h == 0, at(0), at(i)))),
        pl.BlockSpec((1, tile, 1), lambda h, i, *_: (h, at(i), 0)),
        pl.BlockSpec((1, tile, 1), lambda h, i, *_: (h, at(i), 0)),
    ]
    for near, _ in chunks:
        specs += [pl.BlockSpec((near.shape[0], wide), lambda h, i, *_: (0, 0))] * 2
    return specs


def paired(refs, count):
    return [(refs[2 * n], refs[2 * n + 1]) for n in range(count)]


def flat(chunks):
    return [one for pair in chunks for one in pair]


def accumulate(halves, perm, scale, chunks, start, total, dtype=jnp.float32):
    tall = halves[0].shape[1]
    wide = chunks[0][0].shape[1]
    depth = sum(near.shape[0] for near, _ in chunks)
    tile = min(512, tall)
    count = len(chunks)

    def body(*refs):
        kept = refs[-2:]
        out = refs[-3]
        keep(paired(refs[4:], count), kept)
        result = tile_product(refs[:4], kept, pl.program_id(0), start)
        if total is not None:
            result = result + refs[-4][0]
        out[0] = result.astype(dtype)

    place = pl.BlockSpec((1, tile, wide), lambda h, i: (h, i, 0))
    specs = tile_specs(start, depth, chunks, tile, tall // tile, lambda i: i)
    operands = [*halves, perm, scale, *flat(chunks)]
    if total is not None:
        specs.append(place)
        operands.append(total)
    return pl.pallas_call(
        body,
        out_shape=jax.ShapeDtypeStruct((2, tall, wide), dtype),
        grid=(2, tall // tile),
        in_specs=specs,
        out_specs=place,
        scratch_shapes=[pltpu.VMEM((depth, wide), jnp.bfloat16)] * 2,
        input_output_aliases={} if total is None else {len(operands) - 1: 0},
        compiler_params=pltpu.CompilerParams(vmem_limit_bytes=58 * 2**20),
        name="accumulate",
    )(*operands)


def finish(halves, perm, scale, chunks, start, total, late, arrived, factors, features, origin):
    _, tall, wide = total.shape
    depth = sum(near.shape[0] for near, _ in chunks)
    tile = min(512, tall)
    tiles = tall // tile
    count = len(chunks)
    thin = late[0].shape[2]
    width = features.shape[1]

    def body(origin_ref, *refs):
        h = pl.program_id(0)
        keep(paired(refs[4:], count), refs[-2:])
        others = refs[4 + 2 * count :]
        total_ref, here, here_par, there, there_par = others[:5]
        b_own, b_par, perm_c, scale_c, feature_ref, sim_ref, sum_ref = others[5:12]
        index = lax.broadcasted_iota(jnp.int32, (thin, wide), 0)
        g_own = (index + origin_ref[3] == perm_c[...]).astype(jnp.bfloat16)
        g_par = (index + origin_ref[4] == perm_c[...]).astype(jnp.bfloat16)
        moved = dot(there[0], g_own) + dot(there_par[0], g_par)
        result = total_ref[0] + moved * scale_c[...]
        result = result + dot(here[0], b_own[...]) + dot(here_par[0], b_par[...])
        result = result + tile_product(refs[:4], refs[-2:], h, start)
        place = jnp.where(h == 0, origin_ref[0], 1 - origin_ref[0])
        row = origin_ref[1] + place * tall + pl.program_id(1) * tile
        row = row + lax.broadcasted_iota(jnp.int32, result.shape, 0)
        col = origin_ref[2] + lax.broadcasted_iota(jnp.int32, result.shape, 1)
        done = jnp.where(row == col, 1.0, decay_factor * result).astype(jnp.bfloat16)
        sim_ref[...] = done
        sum_ref[...] = dot(done, feature_ref[...])

    def placed(h, i, o):
        return (jnp.where(h == 0, o[0], 1 - o[0]) * tiles + i, 0)

    same = pl.BlockSpec((1, tile, thin), lambda h, i, o: (h, i, 0))
    swapped = pl.BlockSpec((1, tile, thin), lambda h, i, o: (1 - h, i, 0))
    specs = tile_specs(start, depth, chunks, tile, tiles, lambda i: i)
    specs += [pl.BlockSpec((1, tile, wide), lambda h, i, o: (h, i, 0))]
    specs += [same, swapped, same, swapped]
    fixed = [*factors, features]
    specs += [pl.BlockSpec(one.shape, lambda h, i, o: (0, 0)) for one in fixed]
    return pl.pallas_call(
        body,
        out_shape=(
            jax.ShapeDtypeStruct((2 * tall, wide), jnp.bfloat16),
            jax.ShapeDtypeStruct((2 * tall, width), jnp.float32),
        ),
        grid_spec=pltpu.PrefetchScalarGridSpec(
            num_scalar_prefetch=1,
            grid=(2, tiles),
            in_specs=specs,
            out_specs=(pl.BlockSpec((tile, wide), placed), pl.BlockSpec((tile, width), placed)),
            scratch_shapes=[pltpu.VMEM((depth, wide), jnp.bfloat16)] * 2,
        ),
        compiler_params=pltpu.CompilerParams(vmem_limit_bytes=58 * 2**20),
        name="finish",
    )(origin, *halves, perm, scale, *flat(chunks), total, *late, *arrived, *fixed)


def gathered_block(diag_blocks, row_id, block_id, row_count, block_count):
    cols = 2 * block_count
    slice_rows = diag_blocks.shape[0] // row_count
    depth = slice_rows // pieces
    whole = jnp.zeros(diag_blocks.shape, diag_blocks.dtype)
    placed = []
    for n in range(pieces):
        own = part(diag_blocks, row_id * slice_rows + n * depth, depth)
        ups, downs = [own], [own]
        for step in range(1, block_count):
            up_pairs = [(c, c + 2) for c in range(cols - 2) if c // 2 >= step - 1]
            down_pairs = [(c, c - 2) for c in range(2, cols) if c // 2 + step - 1 <= block_count - 1]
            ups.append(lax.ppermute(ups[-1], "col", up_pairs))
            downs.append(lax.ppermute(downs[-1], "col", down_pairs))
        slices = [own] + [ups[j] + downs[block_count - j] for j in range(1, block_count)]
        for distance in range(row_count):
            wanted = row_id ^ distance
            piece = pick(slices, (block_id - wanted) % block_count)
            if distance:
                piece = flipped(piece, "row", distance)
            placed.append((distance, n, piece, wanted * slice_rows + n * depth))
    for _, _, piece, place in sorted(placed, key=lambda entry: entry[0] > 0):
        whole = lax.dynamic_update_slice_in_dim(whole, piece, place, 0)
    return whole


def program(sim, diag_blocks, match_perm, match_scale, features):
    row_count = lax.axis_size("row")
    col_count = lax.axis_size("col")
    block_count = col_count // 2
    row_id = lax.axis_index("row")
    col_id = lax.axis_index("col")
    block_id = col_id // 2
    side = col_id % 2
    rows, half = sim.shape
    other = 1 - side
    bf16 = jnp.bfloat16
    first = half * first_quarters // 4
    spans = [(sum(parts[:n]) * rows // 16, parts[n] * rows // 16) for n in range(len(parts))]

    whole_b = gathered_block(diag_blocks, row_id, block_id, row_count, block_count)
    late_here = sim[:, first:]
    late_far_rows = shifted(late_here, "row", row_count // 2)
    partner = flipped(sim, "col", 1)

    far_block = (block_id + block_count // 2) % block_count
    far_row = (row_id + row_count // 2) % row_count
    perm_c = part(lax.dynamic_index_in_dim(match_perm, far_block, 0, False), side * half, half)
    scale_c = part(lax.dynamic_index_in_dim(match_scale, far_block, 0, False), side * half, half)
    perm_r = lax.dynamic_index_in_dim(match_perm, far_row, 0, False)
    scale_r = lax.dynamic_index_in_dim(match_scale, far_row, 0, False)
    perm_r = jnp.stack([part(perm_r, side * half, half), part(perm_r, other * half, half)])
    scale_r = jnp.stack([part(scale_r, side * half, half), part(scale_r, other * half, half)])
    pick_own = one_hot(side * half, half, perm_c)
    pick_par = one_hot(other * half, half, perm_c)
    pick_own, pick_par = pick_own[:first], pick_par[:first]
    scale_rows = jnp.broadcast_to(scale_c[None, :], (max(d for _, d in spans), half))
    perm_r = perm_r[:, :, None]
    scale_r = scale_r[:, :, None]
    b_own = part(diag_blocks, side * half, half)
    b_par = part(diag_blocks, other * half, half)

    local = dot(sim[:, :first], b_own[:first])
    local = local + dot(partner[:, :first], b_par[:first])
    cuts = [sim[start : start + depth, :first] for start, depth in spans]
    chunks = []
    for n, (start, depth) in enumerate(spans):
        span = slice(start, start + depth)
        got = shifted(cuts[n], "col", col_count // 2)
        got_par = flipped(got, "col", 1)
        moved = dot(got, pick_own) + dot(got_par, pick_par)
        mixed = (local[span] + moved * scale_rows[:depth]).astype(bf16)
        chunks.append((mixed, shifted(mixed, "row", row_count // 2)))

    other_b = flipped(whole_b, "col", 1)
    halves = (whole_b, other_b)
    pair = [(late_here, late_far_rows)]
    late = accumulate(halves, perm_r, scale_r, pair, 0, None, bf16)
    there = shifted(late, "col", col_count // 2)
    late = (late, flipped(late, "col", 1))
    arrived = (there, flipped(there, "col", 1))
    total = None
    for low, high in groups:
        total = accumulate(
            halves, perm_r, scale_r, chunks[low:high], spans[low][0], total
        )

    origin = [side, row_id * rows, col_id * half, side * half + first, other * half + first]
    origin = jnp.stack(origin).astype(jnp.int32)
    factors = (b_own[first:], b_par[first:], perm_c[None, :], scale_c[None, :])
    low = groups[-1][1]
    new_sim, sums = finish(
        halves, perm_r, scale_r, chunks[low:], spans[low][0], total, late, arrived,
        factors, features, origin,
    )
    aggregated = scattered(sums, side, block_id, block_count)
    return new_sim, aggregated


def scattered(total, side, block_id, block_count):
    total = total.reshape(block_count, 2, -1, total.shape[1])
    kept = lax.dynamic_index_in_dim(total, side, 1, False)
    sent = lax.dynamic_index_in_dim(total, 1 - side, 1, False).astype(jnp.bfloat16)
    kept = kept + flipped(sent, "col", 1)
    result = lax.dynamic_index_in_dim(kept, block_id, 0, False)
    for distance in range(1, block_count):
        sent = lax.dynamic_index_in_dim(kept, block_id ^ distance, 0, False)
        result = result + flipped(sent.astype(jnp.bfloat16), "col", 2 * distance)
    return result


def solution(mesh):
    placed = (P("row", "col"), P(None, "col"), P(), P(), P("col", None))
    return jax.shard_map(
        program,
        mesh=mesh,
        in_specs=placed,
        out_specs=(P("row", "col"), P(("row", "col"), None)),
        check_vma=False,
    )
```

```python
import math

import jax
import jax.numpy as jnp
from jax import lax
from jax.experimental import pallas as pl
from jax.experimental.pallas import tpu as pltpu
from jax.sharding import PartitionSpec as P


decay_factor = 0.8
parts = (2,) * 8
groups = ((0, 2), (2, 7))
first_quarters = 3
pieces = 2


def flipped(value, axis, mask):
    pairs = [(source, source ^ mask) for source in range(lax.axis_size(axis))]
    return lax.ppermute(value, axis, pairs)


def shifted(value, axis, steps):
    count = lax.axis_size(axis)
    pairs = [(source, (source + steps) % count) for source in range(count)]
    return lax.ppermute(value, axis, pairs)


def dot(a, b):
    return jnp.dot(a, b, preferred_element_type=jnp.float32)


def dot_t(a, b):
    return lax.dot_general(a, b, (((0,), (0,)), ((), ())), preferred_element_type=jnp.float32)


def one_hot(start, rows, targets):
    index = start + lax.broadcasted_iota(jnp.int32, (rows, targets.shape[0]), 0)
    return (index == targets[None, :]).astype(jnp.bfloat16)


def part(x, start, size, axis=0):
    return lax.dynamic_slice_in_dim(x, start, size, axis)


def pick(items, index):
    result = items[0]
    for position in range(1, len(items)):
        result = jnp.where(index == position, items[position], result)
    return result


def tile_product(refs, kept, h, start):
    b_own, b_par, perm, scale = refs
    b_own, b_par = [jnp.concatenate([one[...] for one in b]) for b in (b_own, b_par)]
    near, far = kept
    shape = (perm.shape[1], near.shape[0])
    index = start + lax.broadcasted_iota(jnp.int32, shape, 1)
    chosen = (index == perm[0]).astype(jnp.bfloat16)
    moved = dot(chosen, far[...]) * scale[0]
    return moved + dot_t(jnp.where(h == 0, b_own, b_par), near[...])


def keep(chunks, kept):
    @pl.when((pl.program_id(0) == 0) & (pl.program_id(1) == 0))
    def _():
        start = 0
        for pair in chunks:
            depth = pair[0].shape[0]
            for one, whole in zip(pair, kept):
                whole[start : start + depth] = one[...]
            start += depth


def tile_specs(start, depth, chunks, tile, tiles, at):
    wide = chunks[0][0].shape[1]
    last = at(tiles - 1)
    unit = math.gcd(start, depth)
    blocks = range(start // unit, (start + depth) // unit)

    def own(block):
        return lambda h, i, *_: (block, jnp.where(h == 0, at(i), last))

    def par(block):
        return lambda h, i, *_: (block, jnp.where(h == 0, at(0), at(i)))

    specs = [pl.BlockSpec((unit, tile), place(block)) for place in (own, par) for block in blocks]
    specs += [
        pl.BlockSpec((1, tile, 1), lambda h, i, *_: (h, at(i), 0)),
        pl.BlockSpec((1, tile, 1), lambda h, i, *_: (h, at(i), 0)),
    ]
    for near, _ in chunks:
        specs += [pl.BlockSpec((near.shape[0], wide), lambda h, i, *_: (0, 0))] * 2
    return specs


def paired(refs, count):
    return [(refs[2 * n], refs[2 * n + 1]) for n in range(count)]


def flat(chunks):
    return [one for pair in chunks for one in pair]


def accumulate(halves, perm, scale, chunks, start, total, dtype=jnp.float32):
    tall = halves[0].shape[1]
    wide = chunks[0][0].shape[1]
    depth = sum(near.shape[0] for near, _ in chunks)
    tile = min(512, tall)
    count = len(chunks)

    blocks = depth // math.gcd(start, depth)

    def body(*refs):
        b, refs = (refs[:blocks], refs[blocks : 2 * blocks]), refs[2 * blocks :]
        kept = refs[-2:]
        out = refs[-3]
        keep(paired(refs[2:], count), kept)
        result = tile_product((*b, *refs[:2]), kept, pl.program_id(0), start)
        if total is not None:
            result = result + refs[-4][0]
        out[0] = result.astype(dtype)

    place = pl.BlockSpec((1, tile, wide), lambda h, i: (h, i, 0))
    specs = tile_specs(start, depth, chunks, tile, tall // tile, lambda i: i)
    operands = [*[halves[0]] * blocks, *[halves[1]] * blocks, perm, scale, *flat(chunks)]
    if total is not None:
        specs.append(place)
        operands.append(total)
    return pl.pallas_call(
        body,
        out_shape=jax.ShapeDtypeStruct((2, tall, wide), dtype),
        grid=(2, tall // tile),
        in_specs=specs,
        out_specs=place,
        scratch_shapes=[pltpu.VMEM((depth, wide), jnp.bfloat16)] * 2,
        input_output_aliases={} if total is None else {len(operands) - 1: 0},
        compiler_params=pltpu.CompilerParams(vmem_limit_bytes=58 * 2**20),
        name="accumulate",
    )(*operands)


def finish(halves, perm, scale, chunks, start, total, late, arrived, factors, features, origin):
    _, tall, wide = total.shape
    depth = sum(near.shape[0] for near, _ in chunks)
    tile = min(512, tall)
    tiles = tall // tile
    count = len(chunks)
    thin = late[0].shape[2]
    width = features.shape[1]

    blocks = depth // math.gcd(start, depth)

    def body(origin_ref, *refs):
        h = pl.program_id(0)
        b, refs = (refs[:blocks], refs[blocks : 2 * blocks]), refs[2 * blocks :]
        keep(paired(refs[2:], count), refs[-2:])
        others = refs[2 + 2 * count :]
        total_ref, here, here_par, there, there_par = others[:5]
        b_own, b_par, perm_c, scale_c, feature_ref, sim_ref, sum_ref = others[5:12]
        index = lax.broadcasted_iota(jnp.int32, (thin, wide), 0)
        g_own = (index + origin_ref[3] == perm_c[...]).astype(jnp.bfloat16)
        g_par = (index + origin_ref[4] == perm_c[...]).astype(jnp.bfloat16)
        moved = dot(there[0], g_own) + dot(there_par[0], g_par)
        result = total_ref[0] + moved * scale_c[...]
        result = result + dot(here[0], b_own[...]) + dot(here_par[0], b_par[...])
        result = result + tile_product((*b, *refs[:2]), refs[-2:], h, start)
        place = jnp.where(h == 0, origin_ref[0], 1 - origin_ref[0])
        row = origin_ref[1] + place * tall + pl.program_id(1) * tile
        row = row + lax.broadcasted_iota(jnp.int32, result.shape, 0)
        col = origin_ref[2] + lax.broadcasted_iota(jnp.int32, result.shape, 1)
        done = jnp.where(row == col, 1.0, decay_factor * result).astype(jnp.bfloat16)
        sim_ref[...] = done
        sum_ref[...] = dot(done, feature_ref[...])

    def placed(h, i, o):
        return (jnp.where(h == 0, o[0], 1 - o[0]) * tiles + i, 0)

    same = pl.BlockSpec((1, tile, thin), lambda h, i, o: (h, i, 0))
    swapped = pl.BlockSpec((1, tile, thin), lambda h, i, o: (1 - h, i, 0))
    specs = tile_specs(start, depth, chunks, tile, tiles, lambda i: i)
    specs += [pl.BlockSpec((1, tile, wide), lambda h, i, o: (h, i, 0))]
    specs += [same, swapped, same, swapped]
    fixed = [*factors, features]
    specs += [pl.BlockSpec(one.shape, lambda h, i, o: (0, 0)) for one in fixed]
    return pl.pallas_call(
        body,
        out_shape=(
            jax.ShapeDtypeStruct((2 * tall, wide), jnp.bfloat16),
            jax.ShapeDtypeStruct((2 * tall, width), jnp.float32),
        ),
        grid_spec=pltpu.PrefetchScalarGridSpec(
            num_scalar_prefetch=1,
            grid=(2, tiles),
            in_specs=specs,
            out_specs=(pl.BlockSpec((tile, wide), placed), pl.BlockSpec((tile, width), placed)),
            scratch_shapes=[pltpu.VMEM((depth, wide), jnp.bfloat16)] * 2,
        ),
        compiler_params=pltpu.CompilerParams(vmem_limit_bytes=58 * 2**20),
        name="finish",
    )(
        origin, *[halves[0]] * blocks, *[halves[1]] * blocks, perm, scale, *flat(chunks),
        total, *late, *arrived, *fixed,
    )


def gathered_block(diag_blocks, row_id, block_id, row_count, block_count):
    cols = 2 * block_count
    slice_rows = diag_blocks.shape[0] // row_count
    depth = slice_rows // pieces
    whole = jnp.zeros(diag_blocks.shape, diag_blocks.dtype)
    placed = []
    for n in range(pieces):
        own = part(diag_blocks, row_id * slice_rows + n * depth, depth)
        ups, downs = [own], [own]
        for step in range(1, block_count):
            up_pairs = [(c, c + 2) for c in range(cols - 2) if c // 2 >= step - 1]
            down_pairs = [(c, c - 2) for c in range(2, cols) if c // 2 + step - 1 <= block_count - 1]
            ups.append(lax.ppermute(ups[-1], "col", up_pairs))
            downs.append(lax.ppermute(downs[-1], "col", down_pairs))
        slices = [own] + [ups[j] + downs[block_count - j] for j in range(1, block_count)]
        for distance in range(row_count):
            wanted = row_id ^ distance
            piece = pick(slices, (block_id - wanted) % block_count)
            if distance:
                piece = flipped(piece, "row", distance)
            placed.append((distance, n, piece, wanted * slice_rows + n * depth))
    for _, _, piece, place in sorted(placed, key=lambda entry: entry[0] > 0):
        whole = lax.dynamic_update_slice_in_dim(whole, piece, place, 0)
    return whole


def program(sim, diag_blocks, match_perm, match_scale, features):
    row_count = lax.axis_size("row")
    col_count = lax.axis_size("col")
    block_count = col_count // 2
    row_id = lax.axis_index("row")
    col_id = lax.axis_index("col")
    block_id = col_id // 2
    side = col_id % 2
    rows, half = sim.shape
    other = 1 - side
    bf16 = jnp.bfloat16
    first = half * first_quarters // 4
    spans = [(sum(parts[:n]) * rows // 16, parts[n] * rows // 16) for n in range(len(parts))]

    whole_b = gathered_block(diag_blocks, row_id, block_id, row_count, block_count)
    late_here = sim[:, first:]
    late_far_rows = shifted(late_here, "row", row_count // 2)
    partner = flipped(sim, "col", 1)

    far_block = (block_id + block_count // 2) % block_count
    far_row = (row_id + row_count // 2) % row_count
    perm_c = part(lax.dynamic_index_in_dim(match_perm, far_block, 0, False), side * half, half)
    scale_c = part(lax.dynamic_index_in_dim(match_scale, far_block, 0, False), side * half, half)
    perm_r = lax.dynamic_index_in_dim(match_perm, far_row, 0, False)
    scale_r = lax.dynamic_index_in_dim(match_scale, far_row, 0, False)
    perm_r = jnp.stack([part(perm_r, side * half, half), part(perm_r, other * half, half)])
    scale_r = jnp.stack([part(scale_r, side * half, half), part(scale_r, other * half, half)])
    pick_own = one_hot(side * half, half, perm_c)
    pick_par = one_hot(other * half, half, perm_c)
    pick_own, pick_par = pick_own[:first], pick_par[:first]
    scale_rows = jnp.broadcast_to(scale_c[None, :], (max(d for _, d in spans), half))
    perm_r = perm_r[:, :, None]
    scale_r = scale_r[:, :, None]
    b_own = part(diag_blocks, side * half, half)
    b_par = part(diag_blocks, other * half, half)

    local = dot(sim[:, :first], b_own[:first])
    local = local + dot(partner[:, :first], b_par[:first])
    cuts = [sim[start : start + depth, :first] for start, depth in spans]
    chunks = []
    for n, (start, depth) in enumerate(spans):
        span = slice(start, start + depth)
        got = shifted(cuts[n], "col", col_count // 2)
        got_par = flipped(got, "col", 1)
        moved = dot(got, pick_own) + dot(got_par, pick_par)
        mixed = (local[span] + moved * scale_rows[:depth]).astype(bf16)
        chunks.append((mixed, shifted(mixed, "row", row_count // 2)))

    other_b = flipped(whole_b, "col", 1)
    halves = (whole_b, other_b)
    pair = [(late_here, late_far_rows)]
    late = accumulate(halves, perm_r, scale_r, pair, 0, None, bf16)
    there = shifted(late, "col", col_count // 2)
    late = (late, flipped(late, "col", 1))
    arrived = (there, flipped(there, "col", 1))
    total = None
    for low, high in groups:
        total = accumulate(
            halves, perm_r, scale_r, chunks[low:high], spans[low][0], total
        )

    origin = [side, row_id * rows, col_id * half, side * half + first, other * half + first]
    origin = jnp.stack(origin).astype(jnp.int32)
    factors = (b_own[first:], b_par[first:], perm_c[None, :], scale_c[None, :])
    low = groups[-1][1]
    new_sim, sums = finish(
        halves, perm_r, scale_r, chunks[low:], spans[low][0], total, late, arrived,
        factors, features, origin,
    )
    aggregated = scattered(sums, side, block_id, block_count)
    return new_sim, aggregated


def scattered(total, side, block_id, block_count):
    total = total.reshape(block_count, 2, -1, total.shape[1])
    kept = lax.dynamic_index_in_dim(total, side, 1, False)
    sent = lax.dynamic_index_in_dim(total, 1 - side, 1, False).astype(jnp.bfloat16)
    kept = kept + flipped(sent, "col", 1)
    result = lax.dynamic_index_in_dim(kept, block_id, 0, False)
    for distance in range(1, block_count):
        sent = lax.dynamic_index_in_dim(kept, block_id ^ distance, 0, False)
        result = result + flipped(sent.astype(jnp.bfloat16), "col", 2 * distance)
    return result


def solution(mesh):
    placed = (P("row", "col"), P(None, "col"), P(), P(), P("col", None))
    return jax.shard_map(
        program,
        mesh=mesh,
        in_specs=placed,
        out_specs=(P("row", "col"), P(("row", "col"), None)),
        check_vma=False,
    )
```
